128 devices in a mesh: sect: 2 (over y_hi), seq: 64 (over z, x, y_lo, core).
Axes of the slice: x: 4, y: 4 (y_hi: 2, y_lo: 2; y = y_hi * 2 + y_lo), z: 4, core: 2. Of those that a mesh axis runs over, the one named last changes fastest.
Arguments:
- queries: bfloat16 [4096, 8192], P('seq'), may hold values from -160 to 160
- key_tokens: bfloat16 [4096, 8192], P('seq'), may hold values from -6 to 6
- value_tokens: bfloat16 [4096, 8192], P('seq'), may hold values from -17 to 17
- latent: bfloat16 [256, 2560], P('seq'), may hold values from -6 to 6
- tile_rows: int32 [64], replicated, may hold values from 1 to 4, 128 in all
- conv_in_weight: bfloat16 [3, 3, 3, 16, 384], replicated, may hold values from -0.3125 to 0.3125
- conv_in_bias: float32 [384], replicated, may hold values from -3 to 3
- norm_gain: float32 [384], replicated, may hold values from 0.5 to 2
- conv_mid_weight: bfloat16 [3, 3, 3, 384, 384], replicated, may hold values from -0.0625 to 0.0625
- conv_mid_bias: float32 [384], replicated, may hold values from -3 to 3
Outputs:
- attended: bfloat16 [4096, 8192], P('seq', 'sect')
- frames: bfloat16 [2, 512, 80, 384], P(None, 'seq', 'sect')
The draws below stay inside these ranges and needn't reach their ends.
Inputs may be any that keep to these rules, and one draw needn't show every extreme that they name: `tile_rows`: the tiles cover the 128 token rows in order; some tile has exactly 4 rows.
All inputs are finite; a program needn't handle non-finite values.
Results may differ from the reference program's by a relative error of at most 0.012.
Values may be sent and summed in bfloat16 or wider, within the bound.
A program may use at most 128 MiB of HBM per device.

```python
import math
import jax
import jax.numpy as jnp
import numpy as np
from jax import lax

DH = 128
CL = 16
CH = 384
LF = 2
MAXT = 4
D = 8192
TOKENS = 4096
GH = 128
GW = 40
N_SEQ = 64


def paired_draw(key):
    first_key, second_key = jax.random.split(jax.random.fold_in(key, 17), 2)
    shape = (TOKENS, D)
    query_part = jnp.clip(jax.random.normal(first_key, shape, jnp.float32), -6.0, 6.0)
    key_part = jnp.clip(jax.random.normal(second_key, shape, jnp.float32), -6.0, 6.0)
    return (query_part, key_part)


def draw_queries(key, part):
    return paired_draw(key)[0].astype(jnp.bfloat16)


def draw_key_tokens(key, part):
    return paired_draw(key)[1].astype(jnp.bfloat16)


def draw_value_tokens(key, part):
    value_key = jax.random.fold_in(jax.random.fold_in(key, 29), 0)
    shape = (TOKENS, D)
    values_drawn = jnp.clip(jax.random.normal(value_key, shape, jnp.float32), -6.0, 6.0)
    return values_drawn.astype(jnp.bfloat16)


def steps_of(rng, shape, cuts, low, largest):
    def one(dim, parts):
        draws = jax.random.uniform(jax.random.fold_in(jax.random.fold_in(rng, 6), dim), (parts,), jnp.float32, low / len(cuts), largest / len(cuts))
        return jnp.repeat(jnp.exp(draws), shape[dim] // parts).reshape((-1,) + (1,) * (len(shape) - dim - 1))

    level = one(*cuts[0])
    for cut in cuts[1:]:
        level = level * one(*cut)
    return level


def split_up(number_of, total, reach, lean):
    weights = [(1 << 20) // math.isqrt(standing ** lean) + 1 for standing in range(2, number_of + 1)]
    spare, counts = total - reach - (number_of - 1), [1] * (number_of - 1)
    while spare > 0:
        candidates = [i for i in range(number_of - 1) if counts[i] < reach]
        mass, left = sum([weights[i] for i in candidates]), spare
        for i in candidates:
            addition = min(reach - counts[i], max(1, left * weights[i] // mass), spare)
            counts[i] = counts[i] + addition
            spare = spare - addition
    return np.array([reach] + counts)


def uneven_parts(stream_key, number_of, total, bound, skew):
    if number_of == 2:
        one = jax.random.randint(stream_key, (), max(1, total - bound), min(bound, total - 1) + 1)
        return jnp.stack([one, total - one])
    lengths = jnp.asarray(split_up(number_of, total, bound, skew), jnp.int32)
    pairs = (number_of - 1) // 2
    source_of, sink = lengths[1:1 + 2 * pairs:2], lengths[2:2 + 2 * pairs:2]
    margin = jnp.minimum(source_of - 1, bound - sink)
    shifted = jax.random.randint(jax.random.fold_in(stream_key, 1), (pairs,), 0, 1 << 20) % (margin + 1)
    lengths = lengths.at[1:1 + 2 * pairs:2].set(source_of - shifted).at[2:2 + 2 * pairs:2].set(sink + shifted)
    return lengths[jax.random.permutation(jax.random.fold_in(stream_key, 2), number_of)]


def noise(rng, extent, deviation, limit, cuts=(), kind=jnp.bfloat16):
    entries = deviation * jax.random.normal(rng, extent, jnp.float32)
    if cuts:
        entries = entries * steps_of(rng, extent, cuts, -0.22, 0.18)
    return jnp.clip(entries, -limit, limit).astype(kind)


def setup_inputs(seed: int = 0) -> dict:
    seeds = jax.random.split(jax.random.key(seed), 11)
    queries = draw_queries(jax.random.fold_in(seeds[10], 71), 0)
    key_tokens = draw_key_tokens(jax.random.fold_in(seeds[10], 71), 0)
    value_tokens = draw_value_tokens(jax.random.fold_in(seeds[10], 71), 0)
    latent = noise(seeds[3], (LF * GH, GW * 4 * CL), 1.0, 6.0, ((0, 64),))
    tile_rows = uneven_parts(seeds[4], N_SEQ, GH, MAXT, 2).astype(jnp.int32)
    conv_in_weight = noise(seeds[5], (3, 3, 3, CL, CH), (27 * CL) ** -0.5, 0.3125)
    conv_in_bias = noise(seeds[6], (CH,), 0.5, 3.0, (), jnp.float32)
    norm_gain = jnp.clip(jnp.exp(jax.random.uniform(seeds[7], (CH,), jnp.float32, math.log(0.5), math.log(2.0))), 0.5, 2.0)
    conv_mid_weight = noise(seeds[8], (3, 3, 3, CH, CH), (27 * CH) ** -0.5, 0.0625)
    conv_mid_bias = noise(seeds[9], (CH,), 0.5, 3.0, (), jnp.float32)
    return dict(queries=queries, key_tokens=key_tokens, value_tokens=value_tokens, latent=latent, tile_rows=tile_rows, conv_in_weight=conv_in_weight, conv_in_bias=conv_in_bias, norm_gain=norm_gain, conv_mid_weight=conv_mid_weight, conv_mid_bias=conv_mid_bias)


def head_attention(query_head, key_head, value_head):
    block_rows = min(512, TOKENS)
    scale_factor = 1.0 / math.sqrt(DH)

    def one_block(query_block):
        scores = jnp.dot(query_block, key_head.T, preferred_element_type=jnp.float32) * scale_factor
        exponents = jnp.exp(scores - lax.optimization_barrier(jnp.max(scores, axis=1, keepdims=True)))
        totals = lax.optimization_barrier(jnp.sum(exponents, axis=1, keepdims=True))
        probabilities = exponents.astype(jnp.bfloat16)
        mixed = jnp.dot(probabilities, value_head, preferred_element_type=jnp.float32) / totals
        return mixed.astype(jnp.bfloat16)
    return lax.map(one_block, query_head.reshape(-1, block_rows, DH)).reshape(TOKENS, DH)

def split_heads(matrix, heads_total):
    return jnp.transpose(matrix.reshape(TOKENS, heads_total, DH), (1, 0, 2))

def causal_conv(field, kernel):
    result = lax.conv_general_dilated(field[None], kernel, (1, 1, 1), [(2, 0), (1, 1), (1, 1)], dimension_numbers=('NDHWC', 'DHWIO', 'NDHWC'), preferred_element_type=jnp.float32)
    return result[0]

def activate(hidden, norm_gain):
    values_wide = hidden.astype(jnp.float32)
    scaled = values_wide * lax.rsqrt(lax.optimization_barrier(jnp.mean(values_wide * values_wide, axis=-1, keepdims=True)) + 1e-06) * norm_gain
    return jax.nn.silu(scaled).astype(jnp.bfloat16)

def reference(queries, key_tokens, value_tokens, latent, tile_rows, conv_in_weight, conv_in_bias, norm_gain, conv_mid_weight, conv_mid_bias):
    heads_total = queries.shape[1] // DH

    def one_head(triple):
        return head_attention(triple[0], triple[1], triple[2])
    per_head = lax.map(one_head, (split_heads(queries, heads_total), split_heads(key_tokens, heads_total), split_heads(value_tokens, heads_total)))
    attended = jnp.transpose(per_head, (1, 0, 2)).reshape(TOKENS, heads_total * DH)
    grid = latent.reshape(LF, GH, GW, 2, 2, CL).transpose(0, 1, 3, 2, 4, 5).reshape(LF, 2 * GH, 2 * GW, CL)
    hidden_first = (causal_conv(grid, conv_in_weight) + conv_in_bias).astype(jnp.bfloat16)
    activated = activate(hidden_first, norm_gain)
    decoded = causal_conv(activated, conv_mid_weight) + conv_mid_bias + hidden_first.astype(jnp.float32)
    tile_starts = (jnp.cumsum(tile_rows) - tile_rows).astype(jnp.int32)
    offsets = jnp.arange(2 * MAXT, dtype=jnp.int32)
    row_index = 2 * tile_starts[:, None] + offsets[None, :]
    inside = offsets[None, :] < 2 * tile_rows[:, None]
    safe_index = jnp.where(inside, row_index, 0).reshape(-1).astype(jnp.int32)
    picked = jnp.take(decoded, safe_index, axis=1)
    frames = jnp.where(inside.reshape(-1)[None, :, None, None], picked, 0.0).astype(jnp.bfloat16)
    return (attended, frames)
```

```python
import functools
import math

import jax
import jax.numpy as jnp
from jax import lax
from jax.experimental import pallas as pl
from jax.experimental.pallas import tpu as pltpu
from jax.sharding import PartitionSpec as P

BF = jnp.bfloat16
F32 = jnp.float32
MESH = pl.DeviceIdType.MESH

DH = 128
ROWS = 64
PEERS = 32
KEYS = 4096
OWN = 2048
BQ = 256
BK = 1024
NB = OWN // BQ
GROUP = 8
GROUPS = PEERS // GROUP
CH = 384
LATW = 1536
LF = 2
OUT_ROWS = 8
COLS = 40
NT = (((1,), (1,)), ((), ()))
EXP2_SCALE = math.log2(math.e) / math.sqrt(DH)


def body(
    tile_rows,
    q,
    k,
    v,
    latent,
    w_in,
    b_in,
    gain,
    w_mid,
    b_mid,
    attended,
    frames,
    kbuf,
    vbuf,
    qbuf,
    obuf,
    vt,
    sbuf,
    mbuf,
    latbuf,
    picked,
    patches,
    win,
    ybuf,
    ring,
    hidden,
    activated,
    wm,
    fbuf,
    s_k,
    s_v,
    s_q,
    s_o,
    s_l,
    r_k,
    r_v,
    r_q,
    r_o,
    r_l,
    fs_k,
    fs_v,
    fs_l,
    fr_k,
    fr_v,
    fr_l,
    w_sem,
    win_sem,
    out_sem,
):
    sect = lax.axis_index("sect")
    me = lax.axis_index("seq")
    core = me % 2
    chip = me // 2
    y = chip % 2
    x = (chip // 2) % 4
    z = chip // 8

    def peer(t, sign=1):
        dz, dx, dy = t // 8, (t // 2) % 4, t % 2
        return (((z + sign * dz + 4) % 4) * 4 + (x + sign * dx + 4) % 4) * 2 + (y + dy) % 2

    def device(other_chip, other_core):
        return (sect, other_chip * 2 + other_core)

    sibling = device(chip, 1 - core)

    def remote(src, dst, send_sem, recv_sem, target):
        return pltpu.make_async_remote_copy(
            src, dst, send_sem, recv_sem, device_id=target, device_id_type=MESH
        )

    barrier = pltpu.get_barrier_semaphore()
    pl.semaphore_signal(barrier, inc=1, device_id=sibling, device_id_type=MESH)

    @pl.loop(1, PEERS)
    def _(t):
        pl.semaphore_signal(barrier, inc=1, device_id=device(peer(t), core), device_id_type=MESH)

    pl.semaphore_wait(barrier, PEERS)

    def head_columns(other_chip):
        return pl.ds(pl.multiple_of((PEERS * sect + other_chip) * DH, DH), DH)

    def slot(t):
        return pl.ds(pl.multiple_of(t * ROWS, ROWS), ROWS)

    def core_slot(t):
        return pl.ds(pl.multiple_of(core * OWN + t * ROWS, ROWS), ROWS)

    def lat_needed(holder, tile_chip):
        low = jnp.maximum(2 * tile_chip, 8 * tile_chip - 128) - 1
        high = jnp.minimum(8 * tile_chip + 4, 65 + 2 * tile_chip) + 4
        first = 8 * (holder % 16)
        return (first + 7 >= low) & (first <= high)

    lat_cols = pl.ds(pl.multiple_of(1024 * sect, 128), LATW)

    @pl.when(lat_needed(chip, chip))
    def _():
        pltpu.make_async_copy(latent.at[:, lat_cols], latbuf.at[core * PEERS], r_l.at[0]).start()

    @pl.loop(1, PEERS)
    def _(t):
        other = peer(t)

        @pl.when(lat_needed(chip, other))
        def _():
            remote(
                latent.at[:, lat_cols],
                latbuf.at[core * PEERS + t],
                s_l.at[t],
                r_l.at[t],
                device(other, core),
            ).start()

    mine = head_columns(chip)
    pltpu.make_async_copy(k.at[:, mine], kbuf.at[core_slot(0)], r_k.at[0]).start()
    pltpu.make_async_copy(v.at[:, mine], vbuf.at[core_slot(0)], r_v.at[0]).start()

    @pl.loop(1, PEERS)
    def _(t):
        other = peer(t)
        target = device(other, core)
        cols = head_columns(other)
        group = t // GROUP
        remote(k.at[:, cols], kbuf.at[core_slot(t)], s_k, r_k.at[group], target).start()
        remote(v.at[:, cols], vbuf.at[core_slot(t)], s_v, r_v.at[group], target).start()

    pltpu.make_async_copy(q.at[:, mine], qbuf.at[slot(0)], r_q.at[0]).start()

    @pl.loop(1, PEERS)
    def _(t):
        other = peer(t)
        remote(
            q.at[:, head_columns(other)], qbuf.at[slot(t)], s_q, r_q.at[t // 4], device(other, core)
        ).start()

    for a in range(1, 3):
        pltpu.make_async_copy(w_mid.at[a], wm.at[a - 1], w_sem).start()
    win[...] = jnp.zeros_like(win)
    for a in range(1, 3):
        for out_p in range(2):
            for out_q in range(2):
                for tap_b in range(3):
                    for tap_e in range(3):
                        cell_r, cell_c = out_p + tap_b, out_q + tap_e
                        far_row, p = (0, cell_r - 1) if cell_r in (1, 2) else (1, 0 if cell_r else 1)
                        far_col, qq = (0, cell_c - 1) if cell_c in (1, 2) else (1, 0 if cell_c else 1)
                        row = (2 - a) * 256 + far_row * 128 + far_col * 64 + p * 32 + qq * 16
                        col = (out_p * 2 + out_q) * CH
                        pltpu.make_async_copy(
                            w_in.at[a, tap_b, tap_e],
                            win.at[row : row + 16, col : col + CH],
                            win_sem,
                        ).start()
    vt[DH:, :] = jnp.ones((16, KEYS), BF)
    ring[...] = jnp.zeros_like(ring)
    picked[...] = jnp.zeros_like(picked)

    def count(d, total):
        return total + jnp.where(d < me, tile_rows[d], 0)

    first_row = lax.fori_loop(0, 64, count, jnp.int32(0))
    filled = tile_rows[me]

    @pl.loop(0, PEERS)
    def _(t):
        @pl.when(lat_needed(peer(t, -1), chip))
        def _():
            here = latbuf.at[core * PEERS + t]
            remote(here, here, fs_l.at[t], r_l.at[t], sibling).wait_recv()
            remote(here, here, fs_l.at[t], fr_l.at[t], sibling).start()

    @pl.loop(0, PEERS)
    def _(t):
        @pl.when(lat_needed(peer(t, -1), chip))
        def _():
            there = latbuf.at[(1 - core) * PEERS + t]
            remote(there, there, fs_l.at[t], fr_l.at[t], sibling).wait_recv()

    def group_rows(which, g):
        return pl.ds(which * OWN + g * GROUP * ROWS, GROUP * ROWS)

    def hand_on(g):
        rows = group_rows(core, g)
        remote(kbuf.at[rows], kbuf.at[rows], fs_k, r_k.at[g], sibling).wait_recv()
        remote(kbuf.at[rows], kbuf.at[rows], fs_k, fr_k.at[g], sibling).start()
        remote(vbuf.at[rows], vbuf.at[rows], fs_v, r_v.at[g], sibling).wait_recv()
        remote(vbuf.at[rows], vbuf.at[rows], fs_v, fr_v.at[g], sibling).start()

    sub_iota = lax.broadcasted_iota(jnp.int32, (4, LATW), 0)
    for f in range(LF):
        for r in range(6):
            g = first_row - 1 + r
            inside = (g >= 0) & (g < 128)
            safe = jnp.clip(g, 0, 127)
            holder = f * 32 + safe // 4
            other = holder // 2
            dz = (z - other // 8 + 4) % 4
            dx = (x - (other // 2) % 4 + 4) % 4
            dy = (y - other % 2 + 2) % 2
            rows4 = latbuf[(holder % 2) * PEERS + dz * 8 + dx * 2 + dy].astype(F32)
            wanted = jnp.where(inside, safe % 4, -1)
            row = jnp.sum(jnp.where(sub_iota == wanted, rows4, 0.0), axis=0, keepdims=True)
            picked[f * 8 + r : f * 8 + r + 1, :] = row

    lane = lax.broadcasted_iota(jnp.int32, (16, 128), 1)
    far = lane >= 64
    p_bit = (lane // 32) % 2
    q_bit = (lane // 16) % 2
    blank = jnp.zeros((16, 128), F32)
    pairs = [picked[:, j * 128 : (j + 1) * 128] for j in range(12)]
    swapped = [pltpu.roll(pair, 64, 1) for pair in pairs]
    for j in range(12):
        before = pairs[j - 1] if j > 0 else blank
        after = swapped[j + 1] if j < 11 else blank
        even = jnp.where(far & (q_bit == 1), before, pairs[j])
        odd = jnp.where(far & (q_bit == 0), after, swapped[j])
        for parity, token in enumerate((even, odd)):
            below = pltpu.roll(token, 15, 0)
            above = pltpu.roll(token, 1, 0)
            rim = jnp.where(p_bit == 0, below, above)
            at = (2 * j + parity) * 16
            patches[at : at + 16, 0:128] = token.astype(BF)
            patches[at : at + 16, 128:256] = rim.astype(BF)
            zero8 = jnp.zeros((8, 128), F32)
            patches[at : at + 16, 256:384] = jnp.concatenate([zero8, token[0:8]], axis=0).astype(BF)
            patches[at : at + 16, 384:512] = jnp.concatenate([zero8, rim[0:8]], axis=0).astype(BF)

    pltpu.make_async_copy(win.at[0:288], win.at[0:288], win_sem).wait()
    for n in range(4):
        conv = jnp.dot(patches[...], win[:, n * CH : (n + 1) * CH], preferred_element_type=F32)
        for part in range(3):
            ybuf[n * 3 + part] = conv[:, part * 128 : (part + 1) * 128]

    hand_on(0)

    bias_in = b_in[...].reshape(1, CH)
    gain_row = gain[...].reshape(1, CH)
    bias_mid = b_mid[...].reshape(1, CH)

    @pl.loop(0, LF)
    def _(f):
        for hr in range(10):
            r, p = (hr + 1) // 2, (hr + 1) % 2
            grid_row = 2 * first_row + hr - 1
            row_valid = (grid_row >= 0) & (grid_row < 256)
            for qq in range(2):
                n = 2 * p + qq
                conv = jnp.concatenate(
                    [ybuf[n * 3 + part, pl.ds(f * 8 + r, 24, stride=16), :] for part in range(3)],
                    axis=1,
                )
                wide = (conv + bias_in).astype(BF).astype(F32)
                mean = jnp.sum(wide * wide, axis=1, keepdims=True) * (1.0 / CH)
                scaled = wide * lax.rsqrt(mean + 1e-6) * gain_row
                act = scaled / (1.0 + jnp.exp(-scaled))
                act = jnp.where(row_valid, act, 0.0)
                for part in range(3):
                    lanes = slice(part * 128, (part + 1) * 128)
                    for e in range(3):
                        ring[e, part, pl.ds(9 - e + qq, 24, stride=2), :] = act[:, lanes]
                    hidden[f, hr, part, pl.ds(qq, 24, stride=2), :] = wide[:, lanes]
            for e in range(3):
                for part in range(3):
                    cut = ring[e, part, pl.ds(pl.multiple_of(8 * sect + 8, 8), COLS), :]
                    at = e * CH + part * 128
                    activated[f, hr * COLS : (hr + 1) * COLS, at : at + 128] = cut.astype(BF)

    hand_on(1)

    pltpu.make_async_copy(wm, wm, w_sem).wait()
    for f in range(LF):
        total = None
        for a in range(3):
            source = f + a - 2
            if source < 0:
                continue
            for b in range(3):
                rows = activated[source, b * COLS : (b + OUT_ROWS) * COLS, :]
                weights = wm[a - 1, b * 3 * CH : (b + 1) * 3 * CH, :]
                part = jnp.dot(rows, weights, preferred_element_type=F32)
                total = part if total is None else total + part
        for ro in range(OUT_ROWS):
            cut = pl.ds(pl.multiple_of(8 * sect, 8), COLS)
            centre = jnp.concatenate(
                [hidden[f, ro + 1, part, cut, :] for part in range(3)], axis=1
            )
            value = total[ro * COLS : (ro + 1) * COLS, :] + bias_mid + centre
            fbuf[f, ro] = jnp.where(ro < 2 * filled, value, 0.0).astype(BF)
        hand_on(2 + f)
    pltpu.make_async_copy(fbuf, frames, out_sem).start()

    for which in range(2):
        for g in range(GROUPS):
            rows = slice(which * OWN + g * GROUP * ROWS, which * OWN + (g + 1) * GROUP * ROWS)

            @pl.when(core != which)
            def _():
                remote(kbuf.at[rows], kbuf.at[rows], fs_k, fr_k.at[g], sibling).wait_recv()
                remote(vbuf.at[rows], vbuf.at[rows], fs_v, fr_v.at[g], sibling).wait_recv()

            vt[0:DH, rows] = vbuf[rows, :].T

    def block(j):
        return pl.ds(pl.multiple_of(j * BQ, BQ), BQ)

    def await_queries(j):
        rows = qbuf.at[block(j)]
        remote(rows, rows, s_q, r_q.at[j], sibling).wait_recv()

    def score_chunk(q_block, which, c, best):
        part = lax.dot_general(
            kbuf[c * BK : (c + 1) * BK, :], q_block, NT, preferred_element_type=F32
        )
        sbuf[which, c * BK : (c + 1) * BK, :] = part
        return jnp.maximum(best, jnp.max(part.reshape(BK // 8, 8, BQ), axis=0))

    def keep_best(best, which):
        top = jnp.max(best, axis=0, keepdims=True) * EXP2_SCALE
        mbuf[which] = jnp.broadcast_to(top, (8, BQ))

    def step(j, with_next):
        which = j % 2
        total = jnp.zeros((DH + 8, BQ), F32)
        if with_next:
            await_queries(j + 1)
            q_next = qbuf[block(j + 1), :]
            best = jnp.full((8, BQ), -jnp.inf, F32)
        top = mbuf[which, 0:1, :]
        for c in range(KEYS // BK):
            if with_next:
                best = score_chunk(q_next, 1 - which, c, best)
            scores = sbuf[which, c * BK : (c + 1) * BK, :]
            weights = jnp.exp2(scores * EXP2_SCALE - top).astype(BF)
            total = total + jnp.dot(
                vt[0 : DH + 8, c * BK : (c + 1) * BK], weights, preferred_element_type=F32
            )
        if with_next:
            keep_best(best, 1 - which)
        obuf[block(j), :] = (total[0:DH, :] / total[DH : DH + 1, :]).T.astype(BF)
        for u in range(BQ // ROWS):
            t = j * (BQ // ROWS) + u

            def send():
                remote(
                    obuf.at[slot(t)], attended.at[:, out_cols], s_o, r_o, device(peer(t, -1), core)
                ).start()

            if u > 0:
                send()
            else:
                pl.when(t > 0)(send)

                @pl.when(t == 0)
                def _():
                    pltpu.make_async_copy(obuf.at[slot(0)], attended.at[:, out_cols], r_o).start()

    out_cols = pl.ds(pl.multiple_of(chip * DH, DH), DH)
    await_queries(0)
    best = jnp.full((8, BQ), -jnp.inf, F32)
    q_first = qbuf[0:BQ, :]
    for c in range(KEYS // BK):
        best = score_chunk(q_first, 0, c, best)
    keep_best(best, 0)

    @pl.loop(0, NB - 1)
    def _(j):
        step(j, True)

    step(jnp.int32(NB - 1), False)

    own = pl.ds(core * OWN, OWN)
    most = kbuf.at[0 : (PEERS - 1) * ROWS]
    remote(most, most, s_k, r_o, sibling).wait_send()
    remote(most, most, s_v, r_o, sibling).wait_send()
    remote(most, most, s_q, r_o, sibling).wait_send()
    remote(kbuf.at[own], kbuf.at[own], fs_k, r_o, sibling).wait_send()
    remote(kbuf.at[own], kbuf.at[own], fs_v, r_o, sibling).wait_send()

    @pl.loop(0, PEERS)
    def _(t):
        @pl.when(lat_needed(peer(t, -1), chip))
        def _():
            here = latbuf.at[core * PEERS + t]
            remote(here, here, fs_l.at[t], r_o, sibling).wait_send()

        @pl.when((t > 0) & lat_needed(chip, peer(t)))
        def _():
            here = latbuf.at[core * PEERS + t]
            remote(here, here, s_l.at[t], r_o, sibling).wait_send()

    pltpu.make_async_copy(fbuf, frames, out_sem).wait()
    remote(most, most, s_o, r_o, sibling).wait_send()
    remote(attended, attended, s_o, r_o, sibling).wait_recv()


def on_device(
    queries,
    key_tokens,
    value_tokens,
    latent,
    tile_rows,
    conv_in_weight,
    conv_in_bias,
    norm_gain,
    conv_mid_weight,
    conv_mid_bias,
):
    dma = pltpu.SemaphoreType.DMA
    anywhere = pl.BlockSpec(memory_space=pl.ANY)
    vmem = pl.BlockSpec(memory_space=pltpu.VMEM)
    smem = pl.BlockSpec(memory_space=pltpu.SMEM)
    return pl.pallas_call(
        body,
        out_shape=(
            jax.ShapeDtypeStruct((ROWS, PEERS * DH), BF),
            jax.ShapeDtypeStruct((LF, OUT_ROWS, COLS, CH), BF),
        ),
        in_specs=[smem] + [anywhere] * 5 + [vmem, vmem, anywhere, vmem],
        out_specs=(anywhere, anywhere),
        scratch_shapes=[
            pltpu.VMEM((KEYS, DH), BF),
            pltpu.VMEM((KEYS, DH), BF),
            pltpu.VMEM((OWN, DH), BF),
            pltpu.VMEM((OWN, DH), BF),
            pltpu.VMEM((DH + 16, KEYS), BF),
            pltpu.VMEM((2, KEYS, BQ), F32),
            pltpu.VMEM((2, 8, BQ), F32),
            pltpu.VMEM((2 * PEERS, 4, LATW), BF),
            pltpu.VMEM((16, LATW), F32),
            pltpu.VMEM((384, 512), BF),
            pltpu.VMEM((512, 4 * CH), BF),
            pltpu.VMEM((12, 384, 128), F32),
            pltpu.VMEM((3, 3, 64, 128), F32),
            pltpu.VMEM((LF, 10, 3, 48, 128), F32),
            pltpu.VMEM((LF, 10 * COLS, 3 * CH), BF),
            pltpu.VMEM((2, 9 * CH, CH), BF),
            pltpu.VMEM((LF, OUT_ROWS, COLS, CH), BF),
            dma,
            dma,
            dma,
            dma,
            dma((PEERS,)),
            dma((GROUPS,)),
            dma((GROUPS,)),
            dma((NB,)),
            dma,
            dma((PEERS,)),
            dma,
            dma,
            dma((PEERS,)),
            dma((GROUPS,)),
            dma((GROUPS,)),
            dma((PEERS,)),
            dma,
            dma,
            dma,
        ],
        compiler_params=pltpu.CompilerParams(
            collective_id=0, has_side_effects=True, vmem_limit_bytes=60 << 20
        ),
        name="attend_and_decode",
    )(
        tile_rows,
        queries,
        key_tokens,
        value_tokens,
        latent,
        conv_in_weight,
        conv_in_bias,
        norm_gain,
        conv_mid_weight.reshape(3, 9 * CH, CH),
        conv_mid_bias,
    )


def solution(mesh):
    in_specs = (P("seq", None),) * 4 + (P(),) * 6
    out_specs = (P("seq", "sect"), P(None, "seq", "sect", None))
    return jax.shard_map(
        on_device, mesh=mesh, in_specs=in_specs, out_specs=out_specs, check_vma=False
    )
```

```python
import functools
import math

import jax
import jax.numpy as jnp
from jax import lax
from jax.experimental import pallas as pl
from jax.experimental.pallas import tpu as pltpu
from jax.sharding import PartitionSpec as P

BF = jnp.bfloat16
F32 = jnp.float32
MESH = pl.DeviceIdType.MESH

DH = 128
ROWS = 64
PEERS = 32
KEYS = 4096
OWN = 2048
BQ = 256
BK = 1024
NB = OWN // BQ
GROUP = 8
GROUPS = PEERS // GROUP
CH = 384
LATW = 1536
LF = 2
OUT_ROWS = 8
COLS = 40
NT = (((1,), (1,)), ((), ()))
EXP2_SCALE = math.log2(math.e) / math.sqrt(DH)


def body(
    tile_rows,
    q,
    k,
    v,
    latent,
    w_in,
    b_in,
    gain,
    w_mid,
    b_mid,
    attended,
    frames,
    kbuf,
    vbuf,
    qbuf,
    obuf,
    vt,
    sbuf,
    mbuf,
    latbuf,
    picked,
    patches,
    win,
    ybuf,
    ring,
    hidden,
    activated,
    wm,
    fbuf,
    s_k,
    s_v,
    s_q,
    s_o,
    s_l,
    r_k,
    r_v,
    r_q,
    r_o,
    r_l,
    fs_k,
    fs_v,
    fs_l,
    fr_k,
    fr_v,
    fr_l,
    w_sem,
    win_sem,
    out_sem,
):
    sect = lax.axis_index("sect")
    me = lax.axis_index("seq")
    core = me % 2
    chip = me // 2
    y = chip % 2
    x = (chip // 2) % 4
    z = chip // 8

    def around(at):
        return jnp.where(at >= 4, at - 4, jnp.where(at < 0, at + 4, at))

    steps_x = {1: [around(x + d) for d in range(4)], -1: [around(x - d) for d in range(4)]}
    steps_y = [y, 1 - y]

    def each_peer(visit, sign=1):
        @pl.loop(0, 4)
        def _(dz):
            peer_z = around(z + sign * dz)
            for rest in range(GROUP):
                visit(dz, rest, peer_z, steps_x[sign][rest // 2] * 2 + steps_y[rest % 2])

    def device(other_chip, other_core):
        return (sect, other_chip * 2 + other_core)

    sibling = device(chip, 1 - core)

    def remote(src, dst, send_sem, recv_sem, target):
        return pltpu.make_async_remote_copy(
            src, dst, send_sem, recv_sem, device_id=target, device_id_type=MESH
        )

    barrier = pltpu.get_barrier_semaphore()
    pl.semaphore_signal(barrier, inc=1, device_id=sibling, device_id_type=MESH)

    def others(act, sign=1):
        def visit(dz, rest, peer_z, low):
            run = functools.partial(act, dz * GROUP + rest, peer_z * 8 + low)
            if rest:
                run()
            else:
                pl.when(dz > 0)(run)

        each_peer(visit, sign)

    def greet(t, other):
        pl.semaphore_signal(barrier, inc=1, device_id=device(other, core), device_id_type=MESH)

    others(greet)

    pl.semaphore_wait(barrier, PEERS)

    def head_columns(other_chip):
        return pl.ds(pl.multiple_of((PEERS * sect + other_chip) * DH, DH), DH)

    def slot(t):
        return pl.ds(pl.multiple_of(t * ROWS, ROWS), ROWS)

    def core_slot(t):
        return pl.ds(pl.multiple_of(core * OWN + t * ROWS, ROWS), ROWS)

    def lat_needed(holder, tile_chip):
        low = jnp.maximum(2 * tile_chip, 8 * tile_chip - 128) - 1
        high = jnp.minimum(8 * tile_chip + 4, 65 + 2 * tile_chip) + 4
        first = 8 * (holder - jnp.where(holder >= 16, 16, 0))
        return (first + 7 >= low) & (first <= high)

    lat_cols = pl.ds(pl.multiple_of(1024 * sect, 128), LATW)

    @pl.when(lat_needed(chip, chip))
    def _():
        pltpu.make_async_copy(latent.at[:, lat_cols], latbuf.at[core * PEERS], r_l.at[0]).start()

    def send_latent(t, other):
        @pl.when(lat_needed(chip, other))
        def _():
            remote(
                latent.at[:, lat_cols],
                latbuf.at[core * PEERS + t],
                s_l.at[t],
                r_l.at[t],
                device(other, core),
            ).start()

    others(send_latent)
    mine = head_columns(chip)
    pltpu.make_async_copy(k.at[:, mine], kbuf.at[core_slot(0)], r_k.at[0]).start()
    pltpu.make_async_copy(v.at[:, mine], vbuf.at[core_slot(0)], r_v.at[0]).start()

    def send_keys(t, other):
        target = device(other, core)
        cols = head_columns(other)
        group = t // GROUP
        remote(k.at[:, cols], kbuf.at[core_slot(t)], s_k, r_k.at[group], target).start()
        remote(v.at[:, cols], vbuf.at[core_slot(t)], s_v, r_v.at[group], target).start()

    others(send_keys)

    for a in range(1, 3):
        pltpu.make_async_copy(w_mid.at[a], wm.at[a - 1], w_sem).start()
    win[...] = jnp.zeros_like(win)
    for a in range(1, 3):
        for out_p in range(2):
            for out_q in range(2):
                for tap_b in range(3):
                    for tap_e in range(3):
                        cell_r, cell_c = out_p + tap_b, out_q + tap_e
                        far_row, p = (0, cell_r - 1) if cell_r in (1, 2) else (1, 0 if cell_r else 1)
                        far_col, qq = (0, cell_c - 1) if cell_c in (1, 2) else (1, 0 if cell_c else 1)
                        row = (2 - a) * 256 + far_row * 128 + far_col * 64 + p * 32 + qq * 16
                        col = (out_p * 2 + out_q) * CH
                        pltpu.make_async_copy(
                            w_in.at[a, tap_b, tap_e],
                            win.at[row : row + 16, col : col + CH],
                            win_sem,
                        ).start()
    vt[DH:, :] = jnp.ones((16, KEYS), BF)
    ring[...] = jnp.zeros_like(ring)
    picked[...] = jnp.zeros_like(picked)

    def count(d, total):
        return total + jnp.where(d < me, tile_rows[d], 0)

    first_row = lax.fori_loop(0, 64, count, jnp.int32(0))
    filled = tile_rows[me]

    def pass_latent(dz, rest, peer_z, low):
        @pl.when(lat_needed(peer_z * 8 + low, chip))
        def _():
            t = dz * GROUP + rest
            here = latbuf.at[core * PEERS + t]
            remote(here, here, fs_l.at[t], r_l.at[t], sibling).wait_recv()
            remote(here, here, fs_l.at[t], fr_l.at[t], sibling).start()

    each_peer(pass_latent, -1)

    def await_latent(dz, rest, peer_z, low):
        @pl.when(lat_needed(peer_z * 8 + low, chip))
        def _():
            t = dz * GROUP + rest
            there = latbuf.at[(1 - core) * PEERS + t]
            remote(there, there, fs_l.at[t], fr_l.at[t], sibling).wait_recv()

    each_peer(await_latent, -1)

    def group_rows(which, g):
        return pl.ds(which * OWN + g * GROUP * ROWS, GROUP * ROWS)

    def hand_on(g):
        rows = group_rows(core, g)
        remote(kbuf.at[rows], kbuf.at[rows], fs_k, r_k.at[g], sibling).wait_recv()
        remote(kbuf.at[rows], kbuf.at[rows], fs_k, fr_k.at[g], sibling).start()
        remote(vbuf.at[rows], vbuf.at[rows], fs_v, r_v.at[g], sibling).wait_recv()
        remote(vbuf.at[rows], vbuf.at[rows], fs_v, fr_v.at[g], sibling).start()

    sub_iota = lax.broadcasted_iota(jnp.int32, (4, LATW), 0)
    for f in range(LF):
        for r in range(6):
            g = first_row - 1 + r
            inside = (g >= 0) & (g < 128)
            safe = jnp.clip(g, 0, 127)
            holder = f * 32 + safe // 4
            other = holder // 2
            dz = (z - other // 8 + 4) % 4
            dx = (x - (other // 2) % 4 + 4) % 4
            dy = (y - other % 2 + 2) % 2
            rows4 = latbuf[(holder % 2) * PEERS + dz * 8 + dx * 2 + dy].astype(F32)
            wanted = jnp.where(inside, safe % 4, -1)
            row = jnp.sum(jnp.where(sub_iota == wanted, rows4, 0.0), axis=0, keepdims=True)
            picked[f * 8 + r : f * 8 + r + 1, :] = row

    lane = lax.broadcasted_iota(jnp.int32, (16, 128), 1)
    far = lane >= 64
    p_bit = (lane // 32) % 2
    q_bit = (lane // 16) % 2
    blank = jnp.zeros((16, 128), F32)
    pairs = [picked[:, j * 128 : (j + 1) * 128] for j in range(12)]
    swapped = [pltpu.roll(pair, 64, 1) for pair in pairs]
    for j in range(12):
        before = pairs[j - 1] if j > 0 else blank
        after = swapped[j + 1] if j < 11 else blank
        even = jnp.where(far & (q_bit == 1), before, pairs[j])
        odd = jnp.where(far & (q_bit == 0), after, swapped[j])
        for parity, token in enumerate((even, odd)):
            below = pltpu.roll(token, 15, 0)
            above = pltpu.roll(token, 1, 0)
            rim = jnp.where(p_bit == 0, below, above)
            at = (2 * j + parity) * 16
            patches[at : at + 16, 0:128] = token.astype(BF)
            patches[at : at + 16, 128:256] = rim.astype(BF)
            zero8 = jnp.zeros((8, 128), F32)
            patches[at : at + 16, 256:384] = jnp.concatenate([zero8, token[0:8]], axis=0).astype(BF)
            patches[at : at + 16, 384:512] = jnp.concatenate([zero8, rim[0:8]], axis=0).astype(BF)

    pltpu.make_async_copy(win.at[0:288], win.at[0:288], win_sem).wait()
    for n in range(4):
        conv = jnp.dot(patches[...], win[:, n * CH : (n + 1) * CH], preferred_element_type=F32)
        for part in range(3):
            ybuf[n * 3 + part] = conv[:, part * 128 : (part + 1) * 128]

    hand_on(0)

    def send_queries():
        pltpu.make_async_copy(q.at[:, mine], qbuf.at[slot(0)], r_q.at[0]).start()

        def send(t, other):
            remote(
                q.at[:, head_columns(other)], qbuf.at[slot(t)], s_q, r_q.at[t // 4], device(other, core)
            ).start()

        others(send)

    bias_in = b_in[...].reshape(1, CH)
    gain_row = gain[...].reshape(1, CH)
    bias_mid = b_mid[...].reshape(1, CH)

    @pl.loop(0, LF)
    def _(f):
        for hr in range(10):
            r, p = (hr + 1) // 2, (hr + 1) % 2
            grid_row = 2 * first_row + hr - 1
            row_valid = (grid_row >= 0) & (grid_row < 256)
            for qq in range(2):
                n = 2 * p + qq
                conv = jnp.concatenate(
                    [ybuf[n * 3 + part, pl.ds(f * 8 + r, 24, stride=16), :] for part in range(3)],
                    axis=1,
                )
                wide = (conv + bias_in).astype(BF).astype(F32)
                mean = jnp.sum(wide * wide, axis=1, keepdims=True) * (1.0 / CH)
                scaled = wide * lax.rsqrt(mean + 1e-6) * gain_row
                act = scaled / (1.0 + jnp.exp(-scaled))
                act = jnp.where(row_valid, act, 0.0)
                for part in range(3):
                    lanes = slice(part * 128, (part + 1) * 128)
                    for e in range(3):
                        ring[e, part, pl.ds(9 - e + qq, 24, stride=2), :] = act[:, lanes]
                    hidden[f, hr, part, pl.ds(qq, 24, stride=2), :] = wide[:, lanes]
            for e in range(3):
                for part in range(3):
                    cut = ring[e, part, pl.ds(pl.multiple_of(8 * sect + 8, 8), COLS), :]
                    at = e * CH + part * 128
                    activated[f, hr * COLS : (hr + 1) * COLS, at : at + 128] = cut.astype(BF)

    hand_on(1)

    pltpu.make_async_copy(wm, wm, w_sem).wait()
    for f in range(LF):
        total = None
        for a in range(3):
            source = f + a - 2
            if source < 0:
                continue
            for b in range(3):
                rows = activated[source, b * COLS : (b + OUT_ROWS) * COLS, :]
                weights = wm[a - 1, b * 3 * CH : (b + 1) * 3 * CH, :]
                part = jnp.dot(rows, weights, preferred_element_type=F32)
                total = part if total is None else total + part
        for ro in range(OUT_ROWS):
            cut = pl.ds(pl.multiple_of(8 * sect, 8), COLS)
            centre = jnp.concatenate(
                [hidden[f, ro + 1, part, cut, :] for part in range(3)], axis=1
            )
            value = total[ro * COLS : (ro + 1) * COLS, :] + bias_mid + centre
            fbuf[f, ro] = jnp.where(ro < 2 * filled, value, 0.0).astype(BF)
        hand_on(2 + f)

        if f == 0:
            send_queries()

    pltpu.make_async_copy(fbuf, frames, out_sem).start()

    for which in range(2):
        for g in range(GROUPS):
            rows = slice(which * OWN + g * GROUP * ROWS, which * OWN + (g + 1) * GROUP * ROWS)

            @pl.when(core != which)
            def _():
                remote(kbuf.at[rows], kbuf.at[rows], fs_k, fr_k.at[g], sibling).wait_recv()
                remote(vbuf.at[rows], vbuf.at[rows], fs_v, fr_v.at[g], sibling).wait_recv()

            vt[0:DH, rows] = vbuf[rows, :].T

    def block(j):
        return pl.ds(pl.multiple_of(j * BQ, BQ), BQ)

    def await_queries(j):
        rows = qbuf.at[block(j)]
        remote(rows, rows, s_q, r_q.at[j], sibling).wait_recv()

    def score_chunk(q_block, which, c, best):
        part = lax.dot_general(
            kbuf[c * BK : (c + 1) * BK, :], q_block, NT, preferred_element_type=F32
        )
        sbuf[which, c * BK : (c + 1) * BK, :] = part
        return jnp.maximum(best, jnp.max(part.reshape(BK // 8, 8, BQ), axis=0))

    def keep_best(best, which):
        top = jnp.max(best, axis=0, keepdims=True) * EXP2_SCALE
        mbuf[which] = jnp.broadcast_to(top, (8, BQ))

    def step(j, which, with_next):
        total = jnp.zeros((DH + 8, BQ), F32)
        if with_next:
            await_queries(j + 1)
            q_next = qbuf[block(j + 1), :]
            best = jnp.full((8, BQ), -jnp.inf, F32)
        top = mbuf[which, 0:1, :]
        for c in range(KEYS // BK):
            if with_next:
                best = score_chunk(q_next, 1 - which, c, best)
            scores = sbuf[which, c * BK : (c + 1) * BK, :]
            weights = jnp.exp2(scores * EXP2_SCALE - top).astype(BF)
            total = total + jnp.dot(
                vt[0 : DH + 8, c * BK : (c + 1) * BK], weights, preferred_element_type=F32
            )
        if with_next:
            keep_best(best, 1 - which)
        obuf[block(j), :] = (total[0:DH, :] / total[DH : DH + 1, :]).T.astype(BF)
        for u in range(BQ // ROWS):
            t = j * (BQ // ROWS) + u

            low = steps_x[-1][2 * which + u // 2] * 2 + steps_y[u % 2]
            other = around(z - (j - which) // 2) * 8 + low

            def send(t=t, other=other):
                remote(
                    obuf.at[slot(t)], attended.at[:, out_cols], s_o, r_o, device(other, core)
                ).start()

            if u > 0 or which:
                send()
            else:
                pl.when(t > 0)(send)

                @pl.when(t == 0)
                def _():
                    pltpu.make_async_copy(obuf.at[slot(0)], attended.at[:, out_cols], r_o).start()

    out_cols = pl.ds(pl.multiple_of(chip * DH, DH), DH)
    await_queries(0)
    best = jnp.full((8, BQ), -jnp.inf, F32)
    q_first = qbuf[0:BQ, :]
    for c in range(KEYS // BK):
        best = score_chunk(q_first, 0, c, best)
    keep_best(best, 0)

    @pl.loop(0, NB // 2 - 1)
    def _(h):
        step(2 * h, 0, True)
        step(2 * h + 1, 1, True)

    step(jnp.int32(NB - 2), 0, True)
    step(jnp.int32(NB - 1), 1, False)

    own = pl.ds(core * OWN, OWN)
    most = kbuf.at[0 : (PEERS - 1) * ROWS]
    remote(most, most, s_k, r_o, sibling).wait_send()
    remote(most, most, s_v, r_o, sibling).wait_send()
    remote(most, most, s_q, r_o, sibling).wait_send()
    remote(kbuf.at[own], kbuf.at[own], fs_k, r_o, sibling).wait_send()
    remote(kbuf.at[own], kbuf.at[own], fs_v, r_o, sibling).wait_send()

    def end_passed(dz, rest, peer_z, low):
        @pl.when(lat_needed(peer_z * 8 + low, chip))
        def _():
            here = latbuf.at[core * PEERS + dz * GROUP + rest]
            remote(here, here, fs_l.at[dz * GROUP + rest], r_o, sibling).wait_send()

    each_peer(end_passed, -1)

    def end_latent(t, other):
        @pl.when(lat_needed(chip, other))
        def _():
            here = latbuf.at[core * PEERS + t]
            remote(here, here, s_l.at[t], r_o, sibling).wait_send()

    others(end_latent)

    pltpu.make_async_copy(fbuf, frames, out_sem).wait()
    remote(most, most, s_o, r_o, sibling).wait_send()
    remote(attended, attended, s_o, r_o, sibling).wait_recv()


def settle(attended_in, frames_in, attended, frames, abuf, fbuf, sems):
    pieces = [(attended_in, abuf, attended, 32 * n, 32) for n in range(2)]
    pieces += [(frames_in, fbuf, frames, n, 1) for n in range(LF)]
    loads, stores = [], []
    for n, (source, staged, target, first, count) in enumerate(pieces):
        part = slice(first, first + count)
        loads.append(pltpu.make_async_copy(source.at[part], staged.at[part], sems.at[0, n]))
        stores.append(pltpu.make_async_copy(staged.at[part], target.at[part], sems.at[1, n]))
    for load in loads:
        load.start()
    for load, store in zip(loads, stores):
        load.wait()
        store.start()
    for store in stores:
        store.wait()


def on_device(
    queries,
    key_tokens,
    value_tokens,
    latent,
    tile_rows,
    conv_in_weight,
    conv_in_bias,
    norm_gain,
    conv_mid_weight,
    conv_mid_bias,
):
    dma = pltpu.SemaphoreType.DMA
    anywhere = pl.BlockSpec(memory_space=pl.ANY)
    vmem = pl.BlockSpec(memory_space=pltpu.VMEM)
    smem = pl.BlockSpec(memory_space=pltpu.SMEM)
    attended, frames = pl.pallas_call(
        body,
        out_shape=(
            jax.ShapeDtypeStruct((ROWS, PEERS * DH), BF),
            jax.ShapeDtypeStruct((LF, OUT_ROWS, COLS, CH), BF),
        ),
        in_specs=[smem] + [anywhere] * 5 + [vmem, vmem, anywhere, vmem],
        out_specs=(anywhere, anywhere),
        scratch_shapes=[
            pltpu.VMEM((KEYS, DH), BF),
            pltpu.VMEM((KEYS, DH), BF),
            pltpu.VMEM((OWN, DH), BF),
            pltpu.VMEM((OWN, DH), BF),
            pltpu.VMEM((DH + 16, KEYS), BF),
            pltpu.VMEM((2, KEYS, BQ), F32),
            pltpu.VMEM((2, 8, BQ), F32),
            pltpu.VMEM((2 * PEERS, 4, LATW), BF),
            pltpu.VMEM((16, LATW), F32),
            pltpu.VMEM((384, 512), BF),
            pltpu.VMEM((512, 4 * CH), BF),
            pltpu.VMEM((12, 384, 128), F32),
            pltpu.VMEM((3, 3, 64, 128), F32),
            pltpu.VMEM((LF, 10, 3, 48, 128), F32),
            pltpu.VMEM((LF, 10 * COLS, 3 * CH), BF),
            pltpu.VMEM((2, 9 * CH, CH), BF),
            pltpu.VMEM((LF, OUT_ROWS, COLS, CH), BF),
            dma,
            dma,
            dma,
            dma,
            dma((PEERS,)),
            dma((GROUPS,)),
            dma((GROUPS,)),
            dma((NB,)),
            dma,
            dma((PEERS,)),
            dma,
            dma,
            dma((PEERS,)),
            dma((GROUPS,)),
            dma((GROUPS,)),
            dma((PEERS,)),
            dma,
            dma,
            dma,
        ],
        compiler_params=pltpu.CompilerParams(
            collective_id=0, has_side_effects=True, vmem_limit_bytes=60 << 20
        ),
        name="attend_and_decode",
    )(
        tile_rows,
        queries,
        key_tokens,
        value_tokens,
        latent,
        conv_in_weight,
        conv_in_bias,
        norm_gain,
        conv_mid_weight.reshape(3, 9 * CH, CH),
        conv_mid_bias,
    )
    return pl.pallas_call(
        settle,
        out_shape=(
            jax.ShapeDtypeStruct(attended.shape, BF),
            jax.ShapeDtypeStruct(frames.shape, BF),
        ),
        in_specs=[anywhere, anywhere],
        out_specs=(anywhere, anywhere),
        scratch_shapes=[
            pltpu.VMEM(attended.shape, BF),
            pltpu.VMEM(frames.shape, BF),
            dma((2, 4)),
        ],
        compiler_params=pltpu.CompilerParams(vmem_limit_bytes=60 << 20),
        name="settle",
    )(attended, frames)


def solution(mesh):
    in_specs = (P("seq", None),) * 4 + (P(),) * 6
    out_specs = (P("seq", "sect"), P(None, "seq", "sect", None))
    return jax.shard_map(
        on_device, mesh=mesh, in_specs=in_specs, out_specs=out_specs, check_vma=False
    )
```

```python
import functools
import math

import jax
import jax.numpy as jnp
from jax import lax
from jax.experimental import pallas as pl
from jax.experimental.pallas import tpu as pltpu
from jax.sharding import PartitionSpec as P

BF = jnp.bfloat16
F32 = jnp.float32
MESH = pl.DeviceIdType.MESH

DH = 128
ROWS = 64
PEERS = 32
KEYS = 4096
OWN = 2048
BQ = 256
BK = 1024
NB = OWN // BQ
GROUP = 8
GROUPS = PEERS // GROUP
CH = 384
LATW = 1536
LF = 2
OUT_ROWS = 8
COLS = 40
NT = (((1,), (1,)), ((), ()))
EXP2_SCALE = math.log2(math.e) / math.sqrt(DH)


def body(
    tile_rows,
    q,
    k,
    v,
    latent,
    w_in,
    b_in,
    gain,
    w_mid,
    b_mid,
    attended,
    frames,
    kbuf,
    vbuf,
    qbuf,
    obuf,
    vt,
    sbuf,
    mbuf,
    latbuf,
    picked,
    patches,
    win,
    ybuf,
    ring,
    hidden,
    activated,
    wm,
    fbuf,
    s_k,
    s_v,
    s_q,
    s_o,
    s_l,
    r_k,
    r_v,
    r_q,
    r_o,
    r_l,
    fs_k,
    fs_v,
    fs_l,
    fr_k,
    fr_v,
    fr_l,
    w_sem,
    win_sem,
    out_sem,
):
    sect = lax.axis_index("sect")
    me = lax.axis_index("seq")
    core = me % 2
    chip = me // 2
    y = chip % 2
    x = (chip // 2) % 4
    z = chip // 8

    def around(at):
        return jnp.where(at >= 4, at - 4, jnp.where(at < 0, at + 4, at))

    steps_z = {1: [around(z + d) for d in range(4)], -1: [around(z - d) for d in range(4)]}
    steps_y = [y, 1 - y]

    def spread(j, u, sign):
        late = j >= 4
        dx = around(jnp.where(late, j - 4, j) + u)
        peer_y = jnp.where(late, steps_y[1 - u % 2], steps_y[u % 2])
        return steps_z[sign][u] * 8 + around(x + sign * dx) * 2 + peer_y

    def each_peer(visit, sign=1):
        @pl.loop(0, NB)
        def _(j):
            for u in range(4):
                visit(j, u, spread(j, u, sign))

    def device(other_chip, other_core):
        return (sect, other_chip * 2 + other_core)

    sibling = device(chip, 1 - core)

    def remote(src, dst, send_sem, recv_sem, target):
        return pltpu.make_async_remote_copy(
            src, dst, send_sem, recv_sem, device_id=target, device_id_type=MESH
        )

    barrier = pltpu.get_barrier_semaphore()
    pl.semaphore_signal(barrier, inc=1, device_id=sibling, device_id_type=MESH)

    def others(act, sign=1):
        def visit(j, u, other):
            run = functools.partial(act, j * 4 + u, other)
            if u:
                run()
            else:
                pl.when(j > 0)(run)

        each_peer(visit, sign)

    def greet(t, other):
        pl.semaphore_signal(barrier, inc=1, device_id=device(other, core), device_id_type=MESH)

    others(greet)

    pl.semaphore_wait(barrier, PEERS)

    def head_columns(other_chip):
        return pl.ds(pl.multiple_of((PEERS * sect + other_chip) * DH, DH), DH)

    def slot(t):
        return pl.ds(pl.multiple_of(t * ROWS, ROWS), ROWS)

    def core_slot(t):
        return pl.ds(pl.multiple_of(core * OWN + t * ROWS, ROWS), ROWS)

    def lat_needed(holder, tile_chip):
        low = jnp.maximum(2 * tile_chip, 8 * tile_chip - 128) - 1
        high = jnp.minimum(8 * tile_chip + 4, 65 + 2 * tile_chip) + 4
        first = 8 * (holder - jnp.where(holder >= 16, 16, 0))
        return (first + 7 >= low) & (first <= high)

    lat_cols = pl.ds(pl.multiple_of(1024 * sect, 128), LATW)

    @pl.when(lat_needed(chip, chip))
    def _():
        pltpu.make_async_copy(latent.at[:, lat_cols], latbuf.at[core * PEERS], r_l.at[0]).start()

    def send_latent(t, other):
        @pl.when(lat_needed(chip, other))
        def _():
            remote(
                latent.at[:, lat_cols],
                latbuf.at[core * PEERS + t],
                s_l.at[t],
                r_l.at[t],
                device(other, core),
            ).start()

    others(send_latent)
    mine = head_columns(chip)
    pltpu.make_async_copy(k.at[:, mine], kbuf.at[core_slot(0)], r_k.at[0]).start()
    pltpu.make_async_copy(v.at[:, mine], vbuf.at[core_slot(0)], r_v.at[0]).start()

    def send_keys(t, other):
        target = device(other, core)
        cols = head_columns(other)
        group = t // GROUP
        remote(k.at[:, cols], kbuf.at[core_slot(t)], s_k, r_k.at[group], target).start()
        remote(v.at[:, cols], vbuf.at[core_slot(t)], s_v, r_v.at[group], target).start()

    others(send_keys)

    for a in range(1, 3):
        pltpu.make_async_copy(w_mid.at[a], wm.at[a - 1], w_sem).start()
    win[...] = jnp.zeros_like(win)
    for a in range(1, 3):
        for out_p in range(2):
            for out_q in range(2):
                for tap_b in range(3):
                    for tap_e in range(3):
                        cell_r, cell_c = out_p + tap_b, out_q + tap_e
                        far_row, p = (0, cell_r - 1) if cell_r in (1, 2) else (1, 0 if cell_r else 1)
                        far_col, qq = (0, cell_c - 1) if cell_c in (1, 2) else (1, 0 if cell_c else 1)
                        row = (2 - a) * 256 + far_row * 128 + far_col * 64 + p * 32 + qq * 16
                        col = (out_p * 2 + out_q) * CH
                        pltpu.make_async_copy(
                            w_in.at[a, tap_b, tap_e],
                            win.at[row : row + 16, col : col + CH],
                            win_sem,
                        ).start()
    vt[DH:, :] = jnp.ones((16, KEYS), BF)
    ring[...] = jnp.zeros_like(ring)
    picked[...] = jnp.zeros_like(picked)

    def count(d, total):
        return total + jnp.where(d < me, tile_rows[d], 0)

    first_row = lax.fori_loop(0, 64, count, jnp.int32(0))
    filled = tile_rows[me]

    def pass_latent(j, u, other):
        @pl.when(lat_needed(other, chip))
        def _():
            t = j * 4 + u
            here = latbuf.at[core * PEERS + t]
            remote(here, here, fs_l.at[t], r_l.at[t], sibling).wait_recv()
            remote(here, here, fs_l.at[t], fr_l.at[t], sibling).start()

    each_peer(pass_latent, -1)

    def await_latent(j, u, other):
        @pl.when(lat_needed(other, chip))
        def _():
            t = j * 4 + u
            there = latbuf.at[(1 - core) * PEERS + t]
            remote(there, there, fs_l.at[t], fr_l.at[t], sibling).wait_recv()

    each_peer(await_latent, -1)

    def group_rows(which, g):
        return pl.ds(which * OWN + g * GROUP * ROWS, GROUP * ROWS)

    def hand_on(g):
        rows = group_rows(core, g)
        remote(kbuf.at[rows], kbuf.at[rows], fs_k, r_k.at[g], sibling).wait_recv()
        remote(kbuf.at[rows], kbuf.at[rows], fs_k, fr_k.at[g], sibling).start()
        remote(vbuf.at[rows], vbuf.at[rows], fs_v, r_v.at[g], sibling).wait_recv()
        remote(vbuf.at[rows], vbuf.at[rows], fs_v, fr_v.at[g], sibling).start()

    sub_iota = lax.broadcasted_iota(jnp.int32, (4, LATW), 0)
    for f in range(LF):
        for r in range(6):
            g = first_row - 1 + r
            inside = (g >= 0) & (g < 128)
            safe = jnp.clip(g, 0, 127)
            holder = f * 32 + safe // 4
            other = holder // 2
            dz = (z - other // 8 + 4) % 4
            dx = (x - (other // 2) % 4 + 4) % 4
            dy = (y - other % 2 + 2) % 2
            turn = (dx - dz + 4) % 4 + 4 * ((dz + dy) % 2)
            rows4 = latbuf[(holder % 2) * PEERS + turn * 4 + dz].astype(F32)
            wanted = jnp.where(inside, safe % 4, -1)
            row = jnp.sum(jnp.where(sub_iota == wanted, rows4, 0.0), axis=0, keepdims=True)
            picked[f * 8 + r : f * 8 + r + 1, :] = row

    lane = lax.broadcasted_iota(jnp.int32, (16, 128), 1)
    far = lane >= 64
    p_bit = (lane // 32) % 2
    q_bit = (lane // 16) % 2
    blank = jnp.zeros((16, 128), F32)
    pairs = [picked[:, j * 128 : (j + 1) * 128] for j in range(12)]
    swapped = [pltpu.roll(pair, 64, 1) for pair in pairs]
    for j in range(12):
        before = pairs[j - 1] if j > 0 else blank
        after = swapped[j + 1] if j < 11 else blank
        even = jnp.where(far & (q_bit == 1), before, pairs[j])
        odd = jnp.where(far & (q_bit == 0), after, swapped[j])
        for parity, token in enumerate((even, odd)):
            below = pltpu.roll(token, 15, 0)
            above = pltpu.roll(token, 1, 0)
            rim = jnp.where(p_bit == 0, below, above)
            at = (2 * j + parity) * 16
            patches[at : at + 16, 0:128] = token.astype(BF)
            patches[at : at + 16, 128:256] = rim.astype(BF)
            zero8 = jnp.zeros((8, 128), F32)
            patches[at : at + 16, 256:384] = jnp.concatenate([zero8, token[0:8]], axis=0).astype(BF)
            patches[at : at + 16, 384:512] = jnp.concatenate([zero8, rim[0:8]], axis=0).astype(BF)

    pltpu.make_async_copy(win.at[0:288], win.at[0:288], win_sem).wait()
    for n in range(4):
        conv = jnp.dot(patches[...], win[:, n * CH : (n + 1) * CH], preferred_element_type=F32)
        for part in range(3):
            ybuf[n * 3 + part] = conv[:, part * 128 : (part + 1) * 128]

    hand_on(0)

    def send_queries():
        pltpu.make_async_copy(q.at[:, mine], qbuf.at[slot(0)], r_q.at[0]).start()

        def send(t, other):
            remote(
                q.at[:, head_columns(other)], qbuf.at[slot(t)], s_q, r_q.at[t // 4], device(other, core)
            ).start()

        others(send)

    bias_in = b_in[...].reshape(1, CH)
    gain_row = gain[...].reshape(1, CH)
    bias_mid = b_mid[...].reshape(1, CH)

    @pl.loop(0, LF)
    def _(f):
        for hr in range(10):
            r, p = (hr + 1) // 2, (hr + 1) % 2
            grid_row = 2 * first_row + hr - 1
            row_valid = (grid_row >= 0) & (grid_row < 256)
            for qq in range(2):
                n = 2 * p + qq
                conv = jnp.concatenate(
                    [ybuf[n * 3 + part, pl.ds(f * 8 + r, 24, stride=16), :] for part in range(3)],
                    axis=1,
                )
                wide = (conv + bias_in).astype(BF).astype(F32)
                mean = jnp.sum(wide * wide, axis=1, keepdims=True) * (1.0 / CH)
                scaled = wide * lax.rsqrt(mean + 1e-6) * gain_row
                act = scaled / (1.0 + jnp.exp(-scaled))
                act = jnp.where(row_valid, act, 0.0)
                for part in range(3):
                    lanes = slice(part * 128, (part + 1) * 128)
                    for e in range(3):
                        ring[e, part, pl.ds(9 - e + qq, 24, stride=2), :] = act[:, lanes]
                    hidden[f, hr, part, pl.ds(qq, 24, stride=2), :] = wide[:, lanes]
            for e in range(3):
                for part in range(3):
                    cut = ring[e, part, pl.ds(pl.multiple_of(8 * sect + 8, 8), COLS), :]
                    at = e * CH + part * 128
                    activated[f, hr * COLS : (hr + 1) * COLS, at : at + 128] = cut.astype(BF)

    hand_on(1)

    pltpu.make_async_copy(wm, wm, w_sem).wait()
    for f in range(LF):
        total = None
        for a in range(3):
            source = f + a - 2
            if source < 0:
                continue
            for b in range(3):
                rows = activated[source, b * COLS : (b + OUT_ROWS) * COLS, :]
                weights = wm[a - 1, b * 3 * CH : (b + 1) * 3 * CH, :]
                part = jnp.dot(rows, weights, preferred_element_type=F32)
                total = part if total is None else total + part
        for ro in range(OUT_ROWS):
            cut = pl.ds(pl.multiple_of(8 * sect, 8), COLS)
            centre = jnp.concatenate(
                [hidden[f, ro + 1, part, cut, :] for part in range(3)], axis=1
            )
            value = total[ro * COLS : (ro + 1) * COLS, :] + bias_mid + centre
            fbuf[f, ro] = jnp.where(ro < 2 * filled, value, 0.0).astype(BF)
        hand_on(2 + f)

        if f == 0:
            send_queries()

    pltpu.make_async_copy(fbuf, frames, out_sem).start()

    for which in range(2):
        for g in range(GROUPS):
            rows = slice(which * OWN + g * GROUP * ROWS, which * OWN + (g + 1) * GROUP * ROWS)

            @pl.when(core != which)
            def _():
                remote(kbuf.at[rows], kbuf.at[rows], fs_k, fr_k.at[g], sibling).wait_recv()
                remote(vbuf.at[rows], vbuf.at[rows], fs_v, fr_v.at[g], sibling).wait_recv()

            vt[0:DH, rows] = vbuf[rows, :].T

    def block(j):
        return pl.ds(pl.multiple_of(j * BQ, BQ), BQ)

    def await_queries(j):
        rows = qbuf.at[block(j)]
        remote(rows, rows, s_q, r_q.at[j], sibling).wait_recv()

    def score_chunk(q_block, which, c, best):
        part = lax.dot_general(
            kbuf[c * BK : (c + 1) * BK, :], q_block, NT, preferred_element_type=F32
        )
        sbuf[which, c * BK : (c + 1) * BK, :] = part
        return jnp.maximum(best, jnp.max(part.reshape(BK // 8, 8, BQ), axis=0))

    def keep_best(best, which):
        top = jnp.max(best, axis=0, keepdims=True) * EXP2_SCALE
        mbuf[which] = jnp.broadcast_to(top, (8, BQ))

    def step(j, which, with_next):
        total = jnp.zeros((DH + 8, BQ), F32)
        if with_next:
            await_queries(j + 1)
            q_next = qbuf[block(j + 1), :]
            best = jnp.full((8, BQ), -jnp.inf, F32)
        top = mbuf[which, 0:1, :]
        for c in range(KEYS // BK):
            if with_next:
                best = score_chunk(q_next, 1 - which, c, best)
            scores = sbuf[which, c * BK : (c + 1) * BK, :]
            weights = jnp.exp2(scores * EXP2_SCALE - top).astype(BF)
            total = total + jnp.dot(
                vt[0 : DH + 8, c * BK : (c + 1) * BK], weights, preferred_element_type=F32
            )
        if with_next:
            keep_best(best, 1 - which)
        obuf[block(j), :] = (total[0:DH, :] / total[DH : DH + 1, :]).T.astype(BF)
        for u in range(BQ // ROWS):
            t = j * (BQ // ROWS) + u

            other = spread(j, u, -1)

            def send(t=t, other=other):
                remote(
                    obuf.at[slot(t)], attended.at[:, out_cols], s_o, r_o, device(other, core)
                ).start()

            if u > 0 or which:
                send()
            else:
                pl.when(t > 0)(send)

                @pl.when(t == 0)
                def _():
                    pltpu.make_async_copy(obuf.at[slot(0)], attended.at[:, out_cols], r_o).start()

    out_cols = pl.ds(pl.multiple_of(chip * DH, DH), DH)
    await_queries(0)
    best = jnp.full((8, BQ), -jnp.inf, F32)
    q_first = qbuf[0:BQ, :]
    for c in range(KEYS // BK):
        best = score_chunk(q_first, 0, c, best)
    keep_best(best, 0)

    @pl.loop(0, NB // 2 - 1)
    def _(h):
        step(2 * h, 0, True)
        step(2 * h + 1, 1, True)

    step(jnp.int32(NB - 2), 0, True)
    step(jnp.int32(NB - 1), 1, False)

    own = pl.ds(core * OWN, OWN)
    most = kbuf.at[0 : (PEERS - 1) * ROWS]
    remote(most, most, s_k, r_o, sibling).wait_send()
    remote(most, most, s_v, r_o, sibling).wait_send()
    remote(most, most, s_q, r_o, sibling).wait_send()
    remote(kbuf.at[own], kbuf.at[own], fs_k, r_o, sibling).wait_send()
    remote(kbuf.at[own], kbuf.at[own], fs_v, r_o, sibling).wait_send()

    def end_passed(j, u, other):
        @pl.when(lat_needed(other, chip))
        def _():
            here = latbuf.at[core * PEERS + j * 4 + u]
            remote(here, here, fs_l.at[j * 4 + u], r_o, sibling).wait_send()

    each_peer(end_passed, -1)

    def end_latent(t, other):
        @pl.when(lat_needed(chip, other))
        def _():
            here = latbuf.at[core * PEERS + t]
            remote(here, here, s_l.at[t], r_o, sibling).wait_send()

    others(end_latent)

    pltpu.make_async_copy(fbuf, frames, out_sem).wait()
    remote(most, most, s_o, r_o, sibling).wait_send()
    remote(attended, attended, s_o, r_o, sibling).wait_recv()


def settle(attended_in, frames_in, attended, frames, abuf, fbuf, sems):
    pieces = [(attended_in, abuf, attended, 32 * n, 32) for n in range(2)]
    pieces += [(frames_in, fbuf, frames, n, 1) for n in range(LF)]
    loads, stores = [], []
    for n, (source, staged, target, first, count) in enumerate(pieces):
        part = slice(first, first + count)
        loads.append(pltpu.make_async_copy(source.at[part], staged.at[part], sems.at[0, n]))
        stores.append(pltpu.make_async_copy(staged.at[part], target.at[part], sems.at[1, n]))
    for load in loads:
        load.start()
    for load, store in zip(loads, stores):
        load.wait()
        store.start()
    for store in stores:
        store.wait()


def on_device(
    queries,
    key_tokens,
    value_tokens,
    latent,
    tile_rows,
    conv_in_weight,
    conv_in_bias,
    norm_gain,
    conv_mid_weight,
    conv_mid_bias,
):
    dma = pltpu.SemaphoreType.DMA
    anywhere = pl.BlockSpec(memory_space=pl.ANY)
    vmem = pl.BlockSpec(memory_space=pltpu.VMEM)
    smem = pl.BlockSpec(memory_space=pltpu.SMEM)
    attended, frames = pl.pallas_call(
        body,
        out_shape=(
            jax.ShapeDtypeStruct((ROWS, PEERS * DH), BF),
            jax.ShapeDtypeStruct((LF, OUT_ROWS, COLS, CH), BF),
        ),
        in_specs=[smem] + [anywhere] * 5 + [vmem, vmem, anywhere, vmem],
        out_specs=(anywhere, anywhere),
        scratch_shapes=[
            pltpu.VMEM((KEYS, DH), BF),
            pltpu.VMEM((KEYS, DH), BF),
            pltpu.VMEM((OWN, DH), BF),
            pltpu.VMEM((OWN, DH), BF),
            pltpu.VMEM((DH + 16, KEYS), BF),
            pltpu.VMEM((2, KEYS, BQ), F32),
            pltpu.VMEM((2, 8, BQ), F32),
            pltpu.VMEM((2 * PEERS, 4, LATW), BF),
            pltpu.VMEM((16, LATW), F32),
            pltpu.VMEM((384, 512), BF),
            pltpu.VMEM((512, 4 * CH), BF),
            pltpu.VMEM((12, 384, 128), F32),
            pltpu.VMEM((3, 3, 64, 128), F32),
            pltpu.VMEM((LF, 10, 3, 48, 128), F32),
            pltpu.VMEM((LF, 10 * COLS, 3 * CH), BF),
            pltpu.VMEM((2, 9 * CH, CH), BF),
            pltpu.VMEM((LF, OUT_ROWS, COLS, CH), BF),
            dma,
            dma,
            dma,
            dma,
            dma((PEERS,)),
            dma((GROUPS,)),
            dma((GROUPS,)),
            dma((NB,)),
            dma,
            dma((PEERS,)),
            dma,
            dma,
            dma((PEERS,)),
            dma((GROUPS,)),
            dma((GROUPS,)),
            dma((PEERS,)),
            dma,
            dma,
            dma,
        ],
        compiler_params=pltpu.CompilerParams(
            collective_id=0, has_side_effects=True, vmem_limit_bytes=60 << 20
        ),
        name="attend_and_decode",
    )(
        tile_rows,
        queries,
        key_tokens,
        value_tokens,
        latent,
        conv_in_weight,
        conv_in_bias,
        norm_gain,
        conv_mid_weight.reshape(3, 9 * CH, CH),
        conv_mid_bias,
    )
    return pl.pallas_call(
        settle,
        out_shape=(
            jax.ShapeDtypeStruct(attended.shape, BF),
            jax.ShapeDtypeStruct(frames.shape, BF),
        ),
        in_specs=[anywhere, anywhere],
        out_specs=(anywhere, anywhere),
        scratch_shapes=[
            pltpu.VMEM(attended.shape, BF),
            pltpu.VMEM(frames.shape, BF),
            dma((2, 4)),
        ],
        compiler_params=pltpu.CompilerParams(vmem_limit_bytes=60 << 20),
        name="settle",
    )(attended, frames)


def solution(mesh):
    in_specs = (P("seq", None),) * 4 + (P(),) * 6
    out_specs = (P("seq", "sect"), P(None, "seq", "sect", None))
    return jax.shard_map(
        on_device, mesh=mesh, in_specs=in_specs, out_specs=out_specs, check_vma=False
    )
```

```python
import functools
import math

import jax
import jax.numpy as jnp
from jax import lax
from jax.experimental import pallas as pl
from jax.experimental.pallas import tpu as pltpu
from jax.sharding import PartitionSpec as P

BF = jnp.bfloat16
F32 = jnp.float32
MESH = pl.DeviceIdType.MESH

DH = 128
ROWS = 64
PEERS = 32
KEYS = 4096
OWN = 2048
BQ = 256
BK = 1024
NB = OWN // BQ
GROUP = 8
GROUPS = PEERS // GROUP
CH = 384
LATW = 1536
LF = 2
OUT_ROWS = 8
COLS = 40
NT = (((1,), (1,)), ((), ()))
EXP2_SCALE = math.log2(math.e) / math.sqrt(DH)


def body(
    tile_rows,
    q,
    k,
    v,
    latent,
    w_in,
    b_in,
    gain,
    w_mid,
    b_mid,
    attended,
    frames,
    kbuf,
    vbuf,
    qbuf,
    obuf,
    vt,
    sbuf,
    mbuf,
    latbuf,
    picked,
    patches,
    win,
    ybuf,
    ring,
    hidden,
    activated,
    wm,
    fbuf,
    s_k,
    s_v,
    s_q,
    s_o,
    s_l,
    r_k,
    r_v,
    r_q,
    r_o,
    r_l,
    fs_k,
    fs_v,
    fs_l,
    fr_k,
    fr_v,
    fr_l,
    w_sem,
    win_sem,
    out_sem,
):
    sect = lax.axis_index("sect")
    me = lax.axis_index("seq")
    core = me % 2
    chip = me // 2
    y = chip % 2
    x = (chip // 2) % 4
    z = chip // 8

    def around(at):
        return jnp.where(at >= 4, at - 4, jnp.where(at < 0, at + 4, at))

    steps_z = {1: [around(z + d) for d in range(4)], -1: [around(z - d) for d in range(4)]}
    steps_y = [y, 1 - y]

    def spread(j, u, sign):
        late = j >= 4
        dx = around(jnp.where(late, j - 4, j) + u)
        peer_y = jnp.where(late, steps_y[1 - u % 2], steps_y[u % 2])
        return steps_z[sign][u] * 8 + around(x + sign * dx) * 2 + peer_y

    def each_peer(visit, sign=1):
        @pl.loop(0, NB)
        def _(j):
            for u in range(4):
                visit(j, u, spread(j, u, sign))

    def device(other_chip, other_core):
        return (sect, other_chip * 2 + other_core)

    sibling = device(chip, 1 - core)

    def remote(src, dst, send_sem, recv_sem, target):
        return pltpu.make_async_remote_copy(
            src, dst, send_sem, recv_sem, device_id=target, device_id_type=MESH
        )

    barrier = pltpu.get_barrier_semaphore()
    pl.semaphore_signal(barrier, inc=1, device_id=sibling, device_id_type=MESH)

    def others(act, sign=1):
        def visit(j, u, other):
            run = functools.partial(act, j * 4 + u, other)
            if u:
                run()
            else:
                pl.when(j > 0)(run)

        each_peer(visit, sign)

    def greet(t, other):
        pl.semaphore_signal(barrier, inc=1, device_id=device(other, core), device_id_type=MESH)

    others(greet)

    pl.semaphore_wait(barrier, PEERS)

    def head_columns(other_chip):
        return pl.ds(pl.multiple_of((PEERS * sect + other_chip) * DH, DH), DH)

    def slot(t):
        return pl.ds(pl.multiple_of(t * ROWS, ROWS), ROWS)

    def core_slot(t):
        return pl.ds(pl.multiple_of(core * OWN + t * ROWS, ROWS), ROWS)

    def lat_needed(holder, tile_chip):
        low = jnp.maximum(2 * tile_chip, 8 * tile_chip - 128) - 1
        high = jnp.minimum(8 * tile_chip + 4, 65 + 2 * tile_chip) + 4
        first = 8 * (holder - jnp.where(holder >= 16, 16, 0))
        return (first + 7 >= low) & (first <= high)

    lat_cols = pl.ds(pl.multiple_of(1024 * sect, 128), LATW)

    @pl.when(lat_needed(chip, chip))
    def _():
        pltpu.make_async_copy(latent.at[:, lat_cols], latbuf.at[core * PEERS], r_l.at[0]).start()

    def send_latent(t, other):
        @pl.when(lat_needed(chip, other))
        def _():
            remote(
                latent.at[:, lat_cols],
                latbuf.at[core * PEERS + t],
                s_l.at[t],
                r_l.at[t],
                device(other, core),
            ).start()

    others(send_latent)
    mine = head_columns(chip)
    pltpu.make_async_copy(k.at[:, mine], kbuf.at[core_slot(0)], r_k.at[0]).start()
    pltpu.make_async_copy(v.at[:, mine], vbuf.at[core_slot(0)], r_v.at[0]).start()

    def send_keys(t, other):
        target = device(other, core)
        cols = head_columns(other)
        group = t // GROUP
        remote(k.at[:, cols], kbuf.at[core_slot(t)], s_k, r_k.at[group], target).start()
        remote(v.at[:, cols], vbuf.at[core_slot(t)], s_v, r_v.at[group], target).start()

    others(send_keys)

    for a in range(1, 3):
        pltpu.make_async_copy(w_mid.at[a], wm.at[a - 1], w_sem).start()
    win[...] = jnp.zeros_like(win)
    for a in range(1, 3):
        for out_p in range(2):
            for out_q in range(2):
                for tap_b in range(3):
                    for tap_e in range(3):
                        cell_r, cell_c = out_p + tap_b, out_q + tap_e
                        far_row, p = (0, cell_r - 1) if cell_r in (1, 2) else (1, 0 if cell_r else 1)
                        far_col, qq = (0, cell_c - 1) if cell_c in (1, 2) else (1, 0 if cell_c else 1)
                        row = (2 - a) * 256 + far_row * 128 + far_col * 64 + p * 32 + qq * 16
                        col = (out_p * 2 + out_q) * CH
                        pltpu.make_async_copy(
                            w_in.at[a, tap_b, tap_e],
                            win.at[row : row + 16, col : col + CH],
                            win_sem,
                        ).start()
    vt[DH:, :] = jnp.ones((16, KEYS), BF)
    ring[...] = jnp.zeros_like(ring)
    picked[...] = jnp.zeros_like(picked)

    def count(d, total):
        return total + jnp.where(d < me, tile_rows[d], 0)

    first_row = lax.fori_loop(0, 64, count, jnp.int32(0))
    filled = tile_rows[me]

    def pass_latent(j, u, other):
        @pl.when(lat_needed(other, chip))
        def _():
            t = j * 4 + u
            here = latbuf.at[core * PEERS + t]
            remote(here, here, fs_l.at[t], r_l.at[t], sibling).wait_recv()
            remote(here, here, fs_l.at[t], fr_l.at[t], sibling).start()

    each_peer(pass_latent, -1)

    def await_latent(j, u, other):
        @pl.when(lat_needed(other, chip))
        def _():
            t = j * 4 + u
            there = latbuf.at[(1 - core) * PEERS + t]
            remote(there, there, fs_l.at[t], fr_l.at[t], sibling).wait_recv()

    each_peer(await_latent, -1)

    def group_rows(which, g):
        return pl.ds(which * OWN + g * GROUP * ROWS, GROUP * ROWS)

    def hand_on(g):
        rows = group_rows(core, g)
        remote(kbuf.at[rows], kbuf.at[rows], fs_k, r_k.at[g], sibling).wait_recv()
        remote(kbuf.at[rows], kbuf.at[rows], fs_k, fr_k.at[g], sibling).start()
        remote(vbuf.at[rows], vbuf.at[rows], fs_v, r_v.at[g], sibling).wait_recv()
        remote(vbuf.at[rows], vbuf.at[rows], fs_v, fr_v.at[g], sibling).start()

    sub_iota = lax.broadcasted_iota(jnp.int32, (4, LATW), 0)
    for f in range(LF):
        for r in range(6):
            g = first_row - 1 + r
            inside = (g >= 0) & (g < 128)
            safe = jnp.clip(g, 0, 127)
            holder = f * 32 + safe // 4
            other = holder // 2
            dz = (z - other // 8 + 4) % 4
            dx = (x - (other // 2) % 4 + 4) % 4
            dy = (y - other % 2 + 2) % 2
            turn = (dx - dz + 4) % 4 + 4 * ((dz + dy) % 2)
            rows4 = latbuf[(holder % 2) * PEERS + turn * 4 + dz].astype(F32)
            wanted = jnp.where(inside, safe % 4, -1)
            row = jnp.sum(jnp.where(sub_iota == wanted, rows4, 0.0), axis=0, keepdims=True)
            picked[f * 8 + r : f * 8 + r + 1, :] = row

    lane = lax.broadcasted_iota(jnp.int32, (16, 128), 1)
    far = lane >= 64
    p_bit = (lane // 32) % 2
    q_bit = (lane // 16) % 2
    blank = jnp.zeros((16, 128), F32)
    pairs = [picked[:, j * 128 : (j + 1) * 128] for j in range(12)]
    swapped = [pltpu.roll(pair, 64, 1) for pair in pairs]
    for j in range(12):
        before = pairs[j - 1] if j > 0 else blank
        after = swapped[j + 1] if j < 11 else blank
        even = jnp.where(far & (q_bit == 1), before, pairs[j])
        odd = jnp.where(far & (q_bit == 0), after, swapped[j])
        for parity, token in enumerate((even, odd)):
            below = pltpu.roll(token, 15, 0)
            above = pltpu.roll(token, 1, 0)
            rim = jnp.where(p_bit == 0, below, above)
            at = (2 * j + parity) * 16
            patches[at : at + 16, 0:128] = token.astype(BF)
            patches[at : at + 16, 128:256] = rim.astype(BF)
            zero8 = jnp.zeros((8, 128), F32)
            patches[at : at + 16, 256:384] = jnp.concatenate([zero8, token[0:8]], axis=0).astype(BF)
            patches[at : at + 16, 384:512] = jnp.concatenate([zero8, rim[0:8]], axis=0).astype(BF)

    pltpu.make_async_copy(win.at[0:288], win.at[0:288], win_sem).wait()
    for n in range(4):
        conv = jnp.dot(patches[...], win[:, n * CH : (n + 1) * CH], preferred_element_type=F32)
        for part in range(3):
            ybuf[n * 3 + part] = conv[:, part * 128 : (part + 1) * 128]

    hand_on(0)

    def send_queries():
        pltpu.make_async_copy(q.at[:, mine], qbuf.at[slot(0)], r_q.at[0]).start()

        def send(t, other):
            remote(
                q.at[:, head_columns(other)], qbuf.at[slot(t)], s_q, r_q.at[t // 4], device(other, core)
            ).start()

        others(send)

    bias_in = b_in[...].reshape(1, CH)
    gain_row = gain[...].reshape(1, CH)
    bias_mid = b_mid[...].reshape(1, CH)

    @pl.loop(0, LF)
    def _(f):
        for hr in range(10):
            r, p = (hr + 1) // 2, (hr + 1) % 2
            grid_row = 2 * first_row + hr - 1
            row_valid = (grid_row >= 0) & (grid_row < 256)
            for qq in range(2):
                n = 2 * p + qq
                conv = jnp.concatenate(
                    [ybuf[n * 3 + part, pl.ds(f * 8 + r, 24, stride=16), :] for part in range(3)],
                    axis=1,
                )
                wide = (conv + bias_in).astype(BF).astype(F32)
                mean = jnp.sum(wide * wide, axis=1, keepdims=True) * (1.0 / CH)
                scaled = wide * lax.rsqrt(mean + 1e-6) * gain_row
                act = scaled / (1.0 + jnp.exp(-scaled))
                act = jnp.where(row_valid, act, 0.0)
                for part in range(3):
                    lanes = slice(part * 128, (part + 1) * 128)
                    for e in range(3):
                        ring[e, part, pl.ds(9 - e + qq, 24, stride=2), :] = act[:, lanes]
                    hidden[f, hr, part, pl.ds(qq, 24, stride=2), :] = wide[:, lanes]
            for e in range(3):
                for part in range(3):
                    cut = ring[e, part, pl.ds(pl.multiple_of(8 * sect + 8, 8), COLS), :]
                    at = e * CH + part * 128
                    activated[f, hr * COLS : (hr + 1) * COLS, at : at + 128] = cut.astype(BF)

    hand_on(1)

    pltpu.make_async_copy(wm, wm, w_sem).wait()
    for f in range(LF):
        total = None
        for a in range(3):
            source = f + a - 2
            if source < 0:
                continue
            for b in range(3):
                rows = activated[source, b * COLS : (b + OUT_ROWS) * COLS, :]
                weights = wm[a - 1, b * 3 * CH : (b + 1) * 3 * CH, :]
                part = jnp.dot(rows, weights, preferred_element_type=F32)
                total = part if total is None else total + part
        for ro in range(OUT_ROWS):
            cut = pl.ds(pl.multiple_of(8 * sect, 8), COLS)
            centre = jnp.concatenate(
                [hidden[f, ro + 1, part, cut, :] for part in range(3)], axis=1
            )
            value = total[ro * COLS : (ro + 1) * COLS, :] + bias_mid + centre
            fbuf[f, ro] = jnp.where(ro < 2 * filled, value, 0.0).astype(BF)
        hand_on(2 + f)

        if f == 0:
            send_queries()

    pltpu.make_async_copy(fbuf, frames, out_sem).start()

    for g in range(GROUPS):
        rows = group_rows(1 - core, g)
        remote(kbuf.at[rows], kbuf.at[rows], fs_k, fr_k.at[g], sibling).wait_recv()

    def block(j):
        return pl.ds(pl.multiple_of(j * BQ, BQ), BQ)

    def await_queries(j):
        rows = qbuf.at[block(j)]
        remote(rows, rows, s_q, r_q.at[j], sibling).wait_recv()

    def score_chunk(q_block, which, c, best):
        part = lax.dot_general(
            kbuf[c * BK : (c + 1) * BK, :], q_block, NT, preferred_element_type=F32
        )
        sbuf[which, c * BK : (c + 1) * BK, :] = part
        return jnp.maximum(best, jnp.max(part.reshape(BK // 8, 8, BQ), axis=0))

    def keep_best(best, which):
        top = jnp.max(best, axis=0, keepdims=True) * EXP2_SCALE
        mbuf[which] = jnp.broadcast_to(top, (8, BQ))

    def step(j, which, with_next):
        total = jnp.zeros((DH + 8, BQ), F32)
        if with_next:
            await_queries(j + 1)
            q_next = qbuf[block(j + 1), :]
            best = jnp.full((8, BQ), -jnp.inf, F32)
        top = mbuf[which, 0:1, :]
        for c in range(KEYS // BK):
            if with_next:
                best = score_chunk(q_next, 1 - which, c, best)
            scores = sbuf[which, c * BK : (c + 1) * BK, :]
            weights = jnp.exp2(scores * EXP2_SCALE - top).astype(BF)
            total = total + jnp.dot(
                vt[0 : DH + 8, c * BK : (c + 1) * BK], weights, preferred_element_type=F32
            )
        if with_next:
            keep_best(best, 1 - which)
        obuf[block(j), :] = (total[0:DH, :] / total[DH : DH + 1, :]).T.astype(BF)
        for u in range(BQ // ROWS):
            t = j * (BQ // ROWS) + u

            other = spread(j, u, -1)

            def send(t=t, other=other):
                remote(
                    obuf.at[slot(t)], attended.at[:, out_cols], s_o, r_o, device(other, core)
                ).start()

            if u > 0 or which:
                send()
            else:
                pl.when(t > 0)(send)

                @pl.when(t == 0)
                def _():
                    pltpu.make_async_copy(obuf.at[slot(0)], attended.at[:, out_cols], r_o).start()

    out_cols = pl.ds(pl.multiple_of(chip * DH, DH), DH)
    await_queries(0)
    best = jnp.full((8, BQ), -jnp.inf, F32)
    q_first = qbuf[0:BQ, :]
    for c in range(KEYS // BK):
        best = score_chunk(q_first, 0, c, best)
    keep_best(best, 0)

    for which in range(2):
        for g in range(GROUPS):
            rows = slice(which * OWN + g * GROUP * ROWS, which * OWN + (g + 1) * GROUP * ROWS)

            @pl.when(core != which)
            def _():
                remote(vbuf.at[rows], vbuf.at[rows], fs_v, fr_v.at[g], sibling).wait_recv()

            vt[0:DH, rows] = vbuf[rows, :].T

    @pl.loop(0, NB // 2 - 1)
    def _(h):
        step(2 * h, 0, True)
        step(2 * h + 1, 1, True)

    step(jnp.int32(NB - 2), 0, True)
    step(jnp.int32(NB - 1), 1, False)

    own = pl.ds(core * OWN, OWN)
    most = kbuf.at[0 : (PEERS - 1) * ROWS]
    remote(most, most, s_k, r_o, sibling).wait_send()
    remote(most, most, s_v, r_o, sibling).wait_send()
    remote(most, most, s_q, r_o, sibling).wait_send()
    remote(kbuf.at[own], kbuf.at[own], fs_k, r_o, sibling).wait_send()
    remote(kbuf.at[own], kbuf.at[own], fs_v, r_o, sibling).wait_send()

    def end_passed(j, u, other):
        @pl.when(lat_needed(other, chip))
        def _():
            here = latbuf.at[core * PEERS + j * 4 + u]
            remote(here, here, fs_l.at[j * 4 + u], r_o, sibling).wait_send()

    each_peer(end_passed, -1)

    def end_latent(t, other):
        @pl.when(lat_needed(chip, other))
        def _():
            here = latbuf.at[core * PEERS + t]
            remote(here, here, s_l.at[t], r_o, sibling).wait_send()

    others(end_latent)

    pltpu.make_async_copy(fbuf, frames, out_sem).wait()
    remote(most, most, s_o, r_o, sibling).wait_send()
    remote(attended, attended, s_o, r_o, sibling).wait_recv()


def settle(attended_in, frames_in, attended, frames, abuf, fbuf, sems):
    pieces = [(attended_in, abuf, attended, 32 * n, 32) for n in range(2)]
    pieces += [(frames_in, fbuf, frames, n, 1) for n in range(LF)]
    loads, stores = [], []
    for n, (source, staged, target, first, count) in enumerate(pieces):
        part = slice(first, first + count)
        loads.append(pltpu.make_async_copy(source.at[part], staged.at[part], sems.at[0, n]))
        stores.append(pltpu.make_async_copy(staged.at[part], target.at[part], sems.at[1, n]))
    for load in loads:
        load.start()
    for load, store in zip(loads, stores):
        load.wait()
        store.start()
    for store in stores:
        store.wait()


def on_device(
    queries,
    key_tokens,
    value_tokens,
    latent,
    tile_rows,
    conv_in_weight,
    conv_in_bias,
    norm_gain,
    conv_mid_weight,
    conv_mid_bias,
):
    dma = pltpu.SemaphoreType.DMA
    anywhere = pl.BlockSpec(memory_space=pl.ANY)
    vmem = pl.BlockSpec(memory_space=pltpu.VMEM)
    smem = pl.BlockSpec(memory_space=pltpu.SMEM)
    attended, frames = pl.pallas_call(
        body,
        out_shape=(
            jax.ShapeDtypeStruct((ROWS, PEERS * DH), BF),
            jax.ShapeDtypeStruct((LF, OUT_ROWS, COLS, CH), BF),
        ),
        in_specs=[smem] + [anywhere] * 5 + [vmem, vmem, anywhere, vmem],
        out_specs=(anywhere, anywhere),
        scratch_shapes=[
            pltpu.VMEM((KEYS, DH), BF),
            pltpu.VMEM((KEYS, DH), BF),
            pltpu.VMEM((OWN, DH), BF),
            pltpu.VMEM((OWN, DH), BF),
            pltpu.VMEM((DH + 16, KEYS), BF),
            pltpu.VMEM((2, KEYS, BQ), F32),
            pltpu.VMEM((2, 8, BQ), F32),
            pltpu.VMEM((2 * PEERS, 4, LATW), BF),
            pltpu.VMEM((16, LATW), F32),
            pltpu.VMEM((384, 512), BF),
            pltpu.VMEM((512, 4 * CH), BF),
            pltpu.VMEM((12, 384, 128), F32),
            pltpu.VMEM((3, 3, 64, 128), F32),
            pltpu.VMEM((LF, 10, 3, 48, 128), F32),
            pltpu.VMEM((LF, 10 * COLS, 3 * CH), BF),
            pltpu.VMEM((2, 9 * CH, CH), BF),
            pltpu.VMEM((LF, OUT_ROWS, COLS, CH), BF),
            dma,
            dma,
            dma,
            dma,
            dma((PEERS,)),
            dma((GROUPS,)),
            dma((GROUPS,)),
            dma((NB,)),
            dma,
            dma((PEERS,)),
            dma,
            dma,
            dma((PEERS,)),
            dma((GROUPS,)),
            dma((GROUPS,)),
            dma((PEERS,)),
            dma,
            dma,
            dma,
        ],
        compiler_params=pltpu.CompilerParams(
            collective_id=0, has_side_effects=True, vmem_limit_bytes=60 << 20
        ),
        name="attend_and_decode",
    )(
        tile_rows,
        queries,
        key_tokens,
        value_tokens,
        latent,
        conv_in_weight,
        conv_in_bias,
        norm_gain,
        conv_mid_weight.reshape(3, 9 * CH, CH),
        conv_mid_bias,
    )
    return pl.pallas_call(
        settle,
        out_shape=(
            jax.ShapeDtypeStruct(attended.shape, BF),
            jax.ShapeDtypeStruct(frames.shape, BF),
        ),
        in_specs=[anywhere, anywhere],
        out_specs=(anywhere, anywhere),
        scratch_shapes=[
            pltpu.VMEM(attended.shape, BF),
            pltpu.VMEM(frames.shape, BF),
            dma((2, 4)),
        ],
        compiler_params=pltpu.CompilerParams(vmem_limit_bytes=60 << 20),
        name="settle",
    )(attended, frames)


def solution(mesh):
    in_specs = (P("seq", None),) * 4 + (P(),) * 6
    out_specs = (P("seq", "sect"), P(None, "seq", "sect", None))
    return jax.shard_map(
        on_device, mesh=mesh, in_specs=in_specs, out_specs=out_specs, check_vma=False
    )
```
